32 devices in a mesh: groups: 2 (over x), wide: 16 (over z, y, core).
Axes of the slice: x: 2, y: 2, z: 4, core: 2. Of those that a mesh axis runs over, the one named last changes fastest.
Arguments:
- frames_in: bfloat16 [128, 256, 768], P(('groups', 'wide')), parts along dimension 0, may hold values from -5 to 5
- qkv_spatial: bfloat16 [768, 2304], replicated, may hold values from -6.5 to 6.5
- out_spatial: bfloat16 [768, 768], replicated, may hold values from -0.21875 to 0.21875
- qkv_temporal: bfloat16 [768, 2304], replicated, may hold values from -6.5 to 6.5
- out_temporal: bfloat16 [768, 768], replicated, may hold values from -0.21875 to 0.21875
Outputs:
- frames_out: bfloat16 [128, 256, 768], P(('groups', 'wide')), parts along dimension 0
The draws below stay inside these ranges and needn't reach their ends.
There are 2 independent parts, one for each index of `groups`. The reference program is written for one: setup_inputs(seed, part) draws one part's arguments, and reference() takes and returns one part's arrays. A program takes and returns all parts, laid end to end along the dimension named above; an argument that names none is the same for every part. Nothing has to cross between parts.
All inputs are finite; a program needn't handle non-finite values.
Results may differ from the reference program's by a relative error of at most 0.008.
Values may be sent and summed in bfloat16 or wider, within the bound.
A program may use at most 128 MiB of HBM per device.

```python
import jax
import jax.numpy as jnp
from jax import lax

D = 768
HEADS = 12
HEAD_DIM = 64
PATCHES = 256
FRAMES = 64


def draw_frames_in(key, part):
    key_base = jax.random.fold_in(key, 11)
    return jnp.clip(jax.random.normal(key_base, (FRAMES, PATCHES, D), jnp.float32), -5.0, 5.0).astype(jnp.bfloat16)


def projection_draw(key):
    inverse = D ** (-0.5)
    key_query = jax.random.fold_in(key, 21)
    key_key = jax.random.fold_in(key, 22)
    key_value = jax.random.fold_in(key, 23)
    queries = jnp.clip(jax.random.normal(key_query, (D, D), jnp.float32), -4.0, 4.0) * inverse
    values = jnp.clip(jax.random.normal(key_value, (D, D), jnp.float32), -4.0, 4.0) * inverse
    other = jnp.clip(jax.random.normal(key_key, (D, D), jnp.float32), -4.0, 4.0) * inverse
    keys_part = other
    return jnp.concatenate([queries, keys_part, values], axis=1)


def draw_qkv_spatial(key, part):
    return projection_draw(jax.random.fold_in(key, 31)).astype(jnp.bfloat16)


def draw_qkv_temporal(key, part):
    return projection_draw(jax.random.fold_in(key, 32)).astype(jnp.bfloat16)


def bell_draw(own_key, dims, width, bound, held_as=jnp.bfloat16):
    entries = width * jax.random.normal(own_key, dims, jnp.float32)
    return jnp.clip(entries, min=-bound, max=bound).astype(held_as)


def setup_inputs(seed: int = 0, part: int = 0) -> dict:
    keys = jax.random.split(jax.random.key(seed), 6)
    part_splits = jax.random.split(jax.random.fold_in(keys[5], part), 6)
    frames_in = draw_frames_in(jax.random.fold_in(jax.random.fold_in(keys[5], part), 71), part)
    qkv_spatial = draw_qkv_spatial(jax.random.fold_in(keys[5], 71), part)
    out_spatial = bell_draw(keys[2], (D, D), D ** -0.5, 0.21875)
    qkv_temporal = draw_qkv_temporal(jax.random.fold_in(keys[5], 71), part)
    out_temporal = bell_draw(keys[4], (D, D), D ** -0.5, 0.21875)
    return {"frames_in": frames_in, "qkv_spatial": qkv_spatial, "out_spatial": out_spatial, "qkv_temporal": qkv_temporal, "out_temporal": out_temporal}


def normalize(tensor):
    floats = tensor.astype(jnp.float32)
    average = lax.optimization_barrier(jnp.mean(floats, axis=-1, keepdims=True))
    centred = floats - average
    spread = lax.optimization_barrier(jnp.mean(centred * centred, axis=-1, keepdims=True))
    return (centred * lax.rsqrt(spread + 1e-06)).astype(jnp.bfloat16)

def attend_sequence(projected):
    length = projected.shape[0]
    split = projected.astype(jnp.float32).reshape(length, 3, HEADS, HEAD_DIM)
    scores = jnp.einsum('qhd,khd->hqk', split[:, 0], split[:, 1]) * HEAD_DIM ** (-0.5)
    weights = jax.nn.softmax(scores, axis=-1).astype(jnp.bfloat16)
    weights = lax.optimization_barrier(weights).astype(jnp.float32)
    mixed = jnp.einsum('hqk,khd->qhd', weights, split[:, 2])
    return mixed.reshape(length, HEADS * HEAD_DIM).astype(jnp.bfloat16)

def reference(frames_in, qkv_spatial, out_spatial, qkv_temporal, out_temporal):
    first = normalize(frames_in)
    proj_one = jnp.dot(first.reshape(-1, D), qkv_spatial, preferred_element_type=jnp.float32)
    proj_one = proj_one.astype(jnp.bfloat16).reshape(FRAMES, PATCHES, 3 * D)
    spatial = lax.map(attend_sequence, proj_one)
    update = jnp.dot(spatial.reshape(-1, D), out_spatial, preferred_element_type=jnp.float32)
    middle = (frames_in.astype(jnp.float32) + update.reshape(FRAMES, PATCHES, D)).astype(jnp.bfloat16)
    second = normalize(middle)
    proj_two = jnp.dot(second.reshape(-1, D), qkv_temporal, preferred_element_type=jnp.float32)
    proj_two = proj_two.astype(jnp.bfloat16).reshape(FRAMES, PATCHES, 3 * D)
    temporal = lax.map(attend_sequence, jnp.swapaxes(proj_two, 0, 1))
    temporal = jnp.swapaxes(temporal, 0, 1)
    change = jnp.dot(temporal.reshape(-1, D), out_temporal, preferred_element_type=jnp.float32)
    return (middle.astype(jnp.float32) + change.reshape(FRAMES, PATCHES, D)).astype(jnp.bfloat16)
```

```python
import functools

import jax
import jax.numpy as jnp
from jax import lax
from jax.experimental import pallas as pl
from jax.experimental.pallas import tpu as pltpu
from jax.sharding import PartitionSpec as P

HEADS = 12
HEAD_DIM = 64


def normalize(tensor):
    floats = tensor.astype(jnp.float32)
    average = jnp.mean(floats, axis=-1, keepdims=True)
    centred = floats - average
    spread = jnp.mean(centred * centred, axis=-1, keepdims=True)
    return (centred * lax.rsqrt(spread + 1e-06)).astype(jnp.bfloat16)


def project(flat_rows, matrix):
    return jnp.dot(flat_rows, matrix, preferred_element_type=jnp.float32)


def attend(projected, score_form, mix_form):
    leading = projected.shape[:-1]
    split = projected.reshape(leading + (3, HEADS, HEAD_DIM))
    queries = split[..., 0, :, :]
    key_part = split[..., 1, :, :]
    values = split[..., 2, :, :]
    scores = jnp.einsum(
        score_form, queries, key_part, preferred_element_type=jnp.float32
    ) * HEAD_DIM ** (-0.5)
    weights = jax.nn.softmax(scores, axis=-1).astype(jnp.bfloat16)
    mixed = jnp.einsum(mix_form, weights, values, preferred_element_type=jnp.float32)
    return mixed.reshape(leading + (HEADS * HEAD_DIM,)).astype(jnp.bfloat16)


def attend_time(received):
    frame_total, single, item_count, columns = received.shape
    sequences = received.reshape(frame_total, item_count, columns)
    result = attend(sequences, "qbhd,kbhd->bhqk", "bhqk,kbhd->qbhd")
    return result.reshape(frame_total, single, item_count, HEADS * HEAD_DIM)


def shards(frames_in, qkv_spatial, out_spatial, qkv_temporal, out_temporal):
    frame_count, patch_count, features = frames_in.shape
    wide_count = lax.axis_size("wide")
    per_group = patch_count // wide_count
    first = normalize(frames_in)
    proj_one = project(first.reshape(-1, features), qkv_spatial).astype(jnp.bfloat16)
    proj_one = proj_one.reshape(frame_count, patch_count, 3 * features)
    spatial = attend(proj_one, "bqhd,bkhd->bhqk", "bhqk,bkhd->bqhd")
    update = project(spatial.reshape(-1, features), out_spatial).reshape(
        frame_count, patch_count, features
    )
    middle = (frames_in.astype(jnp.float32) + update).astype(jnp.bfloat16)
    second = normalize(middle)
    grouped = second.reshape(frame_count, wide_count, per_group, features)
    received = lax.all_to_all(grouped, "wide", split_axis=1, concat_axis=0, tiled=True)
    frame_total, single, item_count, columns = received.shape
    local_proj = project(received.reshape(-1, columns), qkv_temporal).astype(jnp.bfloat16)
    local_proj = local_proj.reshape(frame_total, single, item_count, 3 * columns)
    temporal = attend_time(local_proj)
    returned = lax.all_to_all(temporal, "wide", split_axis=0, concat_axis=1, tiled=True)
    change = project(returned.reshape(-1, features), out_temporal).reshape(
        frame_count, patch_count, features
    )
    return (middle.astype(jnp.float32) + change).astype(jnp.bfloat16)

LOG2E = 1.4426950408889634
MESH = pl.DeviceIdType.MESH
ROWS = 256


def attend_pair(queries, key_part, values, bias):
    lane = lax.broadcasted_iota(jnp.int32, queries.shape, 1)
    low = lane < HEAD_DIM
    zero = jnp.zeros_like(queries)
    one = jnp.ones_like(values)
    halves = []
    for head in range(2):
        keep = low if head == 0 else jnp.logical_not(low)
        scores = lax.dot_general(
            jnp.where(keep, queries, zero),
            key_part,
            (((1,), (1,)), ((), ())),
            preferred_element_type=jnp.float32,
        )
        if bias is not None:
            scores = scores + bias
        top = jnp.max(scores, axis=-1, keepdims=True)
        weights = jnp.exp2(scores - top).astype(jnp.bfloat16)
        halves.append(
            jnp.dot(
                weights,
                jnp.where(keep, values, one),
                preferred_element_type=jnp.float32,
            )
        )
    mixed = jnp.where(low, halves[0], halves[1])
    totals = pltpu.roll(jnp.where(low, halves[1], halves[0]), HEAD_DIM, 1)
    return (mixed / totals).astype(jnp.bfloat16)


def dot32(a, b):
    return jnp.dot(a, b, preferred_element_type=jnp.float32)


def kernel(
    wide,
    frames_hbm, qkv_s_hbm, out_s_hbm, qkv_t_hbm, out_t_hbm,
    result_hbm,
    frames, qkv_s, out_s, qkv_t, out_t,
    first, mixed, middle, second, received, sorted_rows,
    heads_q, heads_k, heads_v, temporal, sending, returned, result,
    load_sem, store_sem, send_one, recv_one, send_two, recv_two,
):
    me = lax.axis_index("wide")
    own, patches, features = frames.shape
    per_group = patches // wide
    band = ROWS // per_group
    bands = own * wide // band
    pair_count = features // 128
    scale = HEAD_DIM ** (-0.5) * LOG2E
    loads = [
        pltpu.make_async_copy(src, dst, load_sem.at[i])
        for i, (src, dst) in enumerate(
            (
                (frames_hbm, frames),
                (qkv_s_hbm, qkv_s),
                (out_s_hbm, out_s),
                (qkv_t_hbm, qkv_t),
                (out_t_hbm, out_t),
            )
        )
    ]
    for load in loads:
        load.start()
    offsets = sorted(range(1, wide), key=lambda o: abs(o - wide // 2))
    barrier = pltpu.get_barrier_semaphore()
    for offset in offsets:
        pl.semaphore_signal(
            barrier, inc=1,
            device_id={"wide": lax.rem(me + offset, wide)}, device_id_type=MESH,
        )
    pl.semaphore_wait(barrier, wide - 1)

    def copy_one(frame, peer):
        return pltpu.make_async_remote_copy(
            src_ref=second.at[frame, peer],
            dst_ref=received.at[me * own + frame],
            send_sem=send_one.at[peer],
            recv_sem=recv_one.at[me],
            device_id={"wide": peer},
            device_id_type=MESH,
        )

    def whole_one(peer):
        return pltpu.make_async_remote_copy(
            src_ref=second.at[:, peer],
            dst_ref=received.at[pl.ds(peer * own, own)],
            send_sem=send_one.at[peer],
            recv_sem=recv_one.at[peer],
            device_id={"wide": peer},
            device_id_type=MESH,
        )

    def copy_two(pair, peer):
        return pltpu.make_async_remote_copy(
            src_ref=sending.at[pair, peer],
            dst_ref=returned.at[pair, me],
            send_sem=send_two.at[peer],
            recv_sem=recv_two.at[me],
            device_id={"wide": peer},
            device_id_type=MESH,
        )

    def whole_two(peer):
        return pltpu.make_async_remote_copy(
            src_ref=sending.at[:, peer],
            dst_ref=returned.at[:, peer],
            send_sem=send_two.at[peer],
            recv_sem=recv_two.at[peer],
            device_id={"wide": peer},
            device_id_type=MESH,
        )

    loads[0].wait()
    loads[1].wait()

    def norm_rows(floats):
        average = jnp.mean(floats, axis=-1, keepdims=True)
        centred = floats - average
        spread = jnp.mean(centred * centred, axis=-1, keepdims=True)
        return (centred * lax.rsqrt(spread + 1e-06)).astype(jnp.bfloat16)

    step_rows = 64

    def one_frame(frame, carry):
        def norm_first(i, c):
            rows = pl.ds(pl.multiple_of(i * step_rows, step_rows), step_rows)
            first[rows, :] = norm_rows(frames[frame, rows, :].astype(jnp.float32))
            return c

        lax.fori_loop(0, patches // step_rows, norm_first, 0)

        def quad(c, carry):
            start = pl.multiple_of(c * 256, 256)
            tokens = first[...]
            queries = (dot32(tokens, qkv_s[:, pl.ds(start, 256)]) * scale).astype(jnp.bfloat16)
            key_part = dot32(
                tokens, qkv_s[:, pl.ds(pl.multiple_of(features + start, 256), 256)]
            ).astype(jnp.bfloat16)
            values = dot32(
                tokens, qkv_s[:, pl.ds(pl.multiple_of(2 * features + start, 256), 256)]
            ).astype(jnp.bfloat16)
            for half in range(2):
                cols = slice(128 * half, 128 * half + 128)
                mixed[:, pl.ds(pl.multiple_of(start + 128 * half, 128), 128)] = attend_pair(
                    queries[:, cols], key_part[:, cols], values[:, cols], None
                )
            return carry

        lax.fori_loop(0, features // 256, quad, 0)

        @pl.when(frame == 0)
        def _():
            loads[2].wait()

        def close(i, c):
            rows = pl.ds(pl.multiple_of(i * step_rows, step_rows), step_rows)
            update = dot32(mixed[rows, :], out_s[...])
            tokens = (frames[frame, rows, :].astype(jnp.float32) + update).astype(jnp.bfloat16)
            middle[frame, rows, :] = tokens
            normed = norm_rows(tokens.astype(jnp.float32))
            count = step_rows // per_group
            second[frame, pl.ds(i * count, count)] = normed.reshape(count, per_group, features)
            return c

        lax.fori_loop(0, patches // step_rows, close, 0)
        received[me * own + frame] = second[frame, me]
        for offset in offsets:
            copy_one(frame, lax.rem(me + offset, wide)).start()
        return carry

    lax.fori_loop(0, own, one_frame, 0)

    row = lax.broadcasted_iota(jnp.int32, (ROWS, ROWS), 0)
    col = lax.broadcasted_iota(jnp.int32, (ROWS, ROWS), 1)
    swap = jnp.where(
        (row // band == col % per_group) & (row % band == col // per_group), 1.0, 0.0
    ).astype(jnp.bfloat16)
    back = jnp.where(
        (col // band == row % per_group) & (col % band == row // per_group), 1.0, 0.0
    ).astype(jnp.bfloat16)
    few = per_group // bands
    bias = jnp.where(
        (row // band) % few == (col // band) % few, 0.0, -1e30
    ).astype(jnp.float32)
    span = few * band

    def arrive(g, carry):
        for j in range(band // own):
            peer = g * (band // own) + j

            @pl.when(peer != me)
            def _():
                whole_one(peer).wait_recv()

        block = received[pl.ds(g * band, band)].reshape(ROWS, features)
        sorted_rows[g] = dot32(swap, block).astype(jnp.bfloat16)
        return carry

    lax.fori_loop(0, bands, arrive, 0)
    loads[3].wait()

    def pair_step(pair, carry):
        start = pl.multiple_of(pair * 128, 128)

        def project_band(g, c):
            tokens = sorted_rows[g]
            matrix = jnp.concatenate(
                [
                    qkv_t[:, pl.ds(pl.multiple_of(part * features + start, 128), 128)]
                    for part in range(3)
                ],
                axis=1,
            )
            out = dot32(tokens, matrix)
            heads_q[g] = (out[:, :128] * scale).astype(jnp.bfloat16)
            heads_k[g] = out[:, 128:256].astype(jnp.bfloat16)
            heads_v[g] = out[:, 256:].astype(jnp.bfloat16)
            return c

        lax.fori_loop(0, bands, project_band, 0)

        def batch(b, c):
            rows = pl.ds(pl.multiple_of(b * span, span), span)
            mix = attend_pair(
                heads_q[:, rows, :].reshape(ROWS, 128),
                heads_k[:, rows, :].reshape(ROWS, 128),
                heads_v[:, rows, :].reshape(ROWS, 128),
                bias,
            )
            temporal[:, rows, :] = mix.reshape(bands, span, 128)
            return c

        lax.fori_loop(0, per_group // few, batch, 0)
        peers = band // own

        def unsort(g, c):
            block = dot32(back, temporal[g]).astype(jnp.bfloat16)
            sending[pair, pl.ds(g * peers, peers)] = block.reshape(peers, own, per_group, 128)
            return c

        lax.fori_loop(0, bands, unsort, 0)
        returned[pair, me] = sending[pair, me]
        for offset in offsets:
            copy_two(pair, lax.rem(me + offset, wide)).start()
        return carry

    lax.fori_loop(0, pair_count, pair_step, 0)
    loads[4].wait()

    def settle(offset, carry):
        peer = lax.rem(me + offset, wide)
        whole_two(peer).wait_recv()
        return carry

    lax.fori_loop(1, wide, settle, 0)

    def finish(frame, carry):
        block = jnp.concatenate(
            [returned[pair, :, frame].reshape(patches, 128) for pair in range(pair_count)],
            axis=1,
        )
        change = dot32(block, out_t[...])
        result[frame] = (middle[frame].astype(jnp.float32) + change).astype(jnp.bfloat16)
        pltpu.make_async_copy(result.at[frame], result_hbm.at[frame], store_sem.at[frame]).start()
        return carry

    lax.fori_loop(0, own, finish, 0)

    def drain(offset, carry):
        peer = lax.rem(me + offset, wide)
        whole_one(peer).wait_send()
        whole_two(peer).wait_send()
        return carry

    lax.fori_loop(1, wide, drain, 0)

    def stored(frame, carry):
        pltpu.make_async_copy(result.at[frame], result_hbm.at[frame], store_sem.at[frame]).wait()
        return carry

    lax.fori_loop(0, own, stored, 0)


def fused(frames_in, qkv_spatial, out_spatial, qkv_temporal, out_temporal):
    own, patches, features = frames_in.shape
    wide = lax.axis_size("wide")
    per_group = patches // wide
    band = ROWS // per_group
    bands = own * wide // band
    pairs = features // 128
    bf16 = jnp.bfloat16
    vmem = pltpu.VMEM
    anywhere = pl.BlockSpec(memory_space=pl.ANY)
    return pl.pallas_call(
        functools.partial(kernel, wide),
        out_shape=jax.ShapeDtypeStruct(frames_in.shape, bf16),
        in_specs=[anywhere] * 5,
        out_specs=anywhere,
        scratch_shapes=[
            vmem(frames_in.shape, bf16),
            vmem(qkv_spatial.shape, bf16),
            vmem(out_spatial.shape, bf16),
            vmem(qkv_temporal.shape, bf16),
            vmem(out_temporal.shape, bf16),
            vmem((patches, features), bf16),
            vmem((patches, features), bf16),
            vmem((own, patches, features), bf16),
            vmem((own, wide, per_group, features), bf16),
            vmem((own * wide, per_group, features), bf16),
            vmem((bands, ROWS, features), bf16),
            vmem((bands, ROWS, 128), bf16),
            vmem((bands, ROWS, 128), bf16),
            vmem((bands, ROWS, 128), bf16),
            vmem((bands, ROWS, 128), bf16),
            vmem((pairs, wide, own, per_group, 128), bf16),
            vmem((pairs, wide, own, per_group, 128), bf16),
            vmem((own, patches, features), bf16),
            pltpu.SemaphoreType.DMA((5,)),
            pltpu.SemaphoreType.DMA((own,)),
            pltpu.SemaphoreType.DMA((wide,)),
            pltpu.SemaphoreType.DMA((wide,)),
            pltpu.SemaphoreType.DMA((wide,)),
            pltpu.SemaphoreType.DMA((wide,)),
        ],
        compiler_params=pltpu.CompilerParams(
            collective_id=0, has_side_effects=True, vmem_limit_bytes=60000 * 1024
        ),
    )(frames_in, qkv_spatial, out_spatial, qkv_temporal, out_temporal)


def fits(frames_in, wide):
    own, patches, features = frames_in.shape
    per_group = patches // wide
    if patches != ROWS or features % 256 or per_group % 16 or ROWS % per_group:
        return False
    band = ROWS // per_group
    return band % own == 0 and (own * wide) % band == 0 and per_group % (own * wide // band) == 0


def pick(frames_in, *matrices):
    if fits(frames_in, lax.axis_size("wide")):
        return fused(frames_in, *matrices)
    return shards(frames_in, *matrices)


def solution(mesh):
    return jax.shard_map(
        pick,
        mesh=mesh,
        in_specs=(P(("groups", "wide"), None, None), P(), P(), P(), P()),
        out_specs=P(("groups", "wide"), None, None),
        check_vma=False,
    )
```

```python
import functools

import jax
import jax.numpy as jnp
from jax import lax
from jax.experimental import pallas as pl
from jax.experimental.pallas import tpu as pltpu
from jax.sharding import PartitionSpec as P

HEADS = 12
HEAD_DIM = 64


def normalize(tensor):
    floats = tensor.astype(jnp.float32)
    average = jnp.mean(floats, axis=-1, keepdims=True)
    centred = floats - average
    spread = jnp.mean(centred * centred, axis=-1, keepdims=True)
    return (centred * lax.rsqrt(spread + 1e-06)).astype(jnp.bfloat16)


def project(flat_rows, matrix):
    return jnp.dot(flat_rows, matrix, preferred_element_type=jnp.float32)


def attend(projected, score_form, mix_form):
    leading = projected.shape[:-1]
    split = projected.reshape(leading + (3, HEADS, HEAD_DIM))
    queries = split[..., 0, :, :]
    key_part = split[..., 1, :, :]
    values = split[..., 2, :, :]
    scores = jnp.einsum(
        score_form, queries, key_part, preferred_element_type=jnp.float32
    ) * HEAD_DIM ** (-0.5)
    weights = jax.nn.softmax(scores, axis=-1).astype(jnp.bfloat16)
    mixed = jnp.einsum(mix_form, weights, values, preferred_element_type=jnp.float32)
    return mixed.reshape(leading + (HEADS * HEAD_DIM,)).astype(jnp.bfloat16)


def attend_time(received):
    frame_total, single, item_count, columns = received.shape
    sequences = received.reshape(frame_total, item_count, columns)
    result = attend(sequences, "qbhd,kbhd->bhqk", "bhqk,kbhd->qbhd")
    return result.reshape(frame_total, single, item_count, HEADS * HEAD_DIM)


def shards(frames_in, qkv_spatial, out_spatial, qkv_temporal, out_temporal):
    frame_count, patch_count, features = frames_in.shape
    wide_count = lax.axis_size("wide")
    per_group = patch_count // wide_count
    first = normalize(frames_in)
    proj_one = project(first.reshape(-1, features), qkv_spatial).astype(jnp.bfloat16)
    proj_one = proj_one.reshape(frame_count, patch_count, 3 * features)
    spatial = attend(proj_one, "bqhd,bkhd->bhqk", "bhqk,bkhd->bqhd")
    update = project(spatial.reshape(-1, features), out_spatial).reshape(
        frame_count, patch_count, features
    )
    middle = (frames_in.astype(jnp.float32) + update).astype(jnp.bfloat16)
    second = normalize(middle)
    grouped = second.reshape(frame_count, wide_count, per_group, features)
    received = lax.all_to_all(grouped, "wide", split_axis=1, concat_axis=0, tiled=True)
    frame_total, single, item_count, columns = received.shape
    local_proj = project(received.reshape(-1, columns), qkv_temporal).astype(jnp.bfloat16)
    local_proj = local_proj.reshape(frame_total, single, item_count, 3 * columns)
    temporal = attend_time(local_proj)
    returned = lax.all_to_all(temporal, "wide", split_axis=0, concat_axis=1, tiled=True)
    change = project(returned.reshape(-1, features), out_temporal).reshape(
        frame_count, patch_count, features
    )
    return (middle.astype(jnp.float32) + change).astype(jnp.bfloat16)

LOG2E = 1.4426950408889634
MESH = pl.DeviceIdType.MESH
ROWS = 256


def attend_pair(queries, key_part, values, bias):
    low = lax.broadcasted_iota(jnp.int32, queries.shape, 1) < HEAD_DIM
    zero = jnp.zeros_like(queries)
    stacked = jnp.concatenate(
        [jnp.where(low, queries, zero), jnp.where(low, zero, queries)], axis=0
    )
    scores = lax.dot_general(
        stacked, key_part, (((1,), (1,)), ((), ())), preferred_element_type=jnp.float32
    )
    if bias is not None:
        scores = scores + bias
    top = jnp.max(scores, axis=-1, keepdims=True)
    weights = jnp.exp2(scores - top).astype(jnp.bfloat16)
    both = dot32(weights, jnp.concatenate([values, jnp.ones_like(values)], axis=1))
    count = queries.shape[0]
    mixed = jnp.where(low, both[:count, :128], both[count:, :128])
    totals = jnp.where(low, both[:count, 128:], both[count:, 128:])
    return (mixed / totals).astype(jnp.bfloat16)


def dot32(a, b):
    return jnp.dot(a, b, preferred_element_type=jnp.float32)


def kernel(
    wide,
    frames_hbm, qkv_s_hbm, out_s_hbm, qkv_t_hbm, out_t_hbm,
    result_hbm,
    frames, qkv_s, out_s, qkv_t, out_t,
    first, mixed, middle, second, received, sorted_rows,
    heads_q, heads_k, heads_v, temporal, sending, returned, result,
    load_sem, store_sem, send_one, recv_one, send_two, recv_two,
):
    me = lax.axis_index("wide")
    own, patches, features = frames.shape
    per_group = patches // wide
    band = ROWS // per_group
    bands = own * wide // band
    pair_count = features // 128
    scale = HEAD_DIM ** (-0.5) * LOG2E
    loads = [
        pltpu.make_async_copy(src, dst, load_sem.at[i])
        for i, (src, dst) in enumerate(
            (
                (frames_hbm, frames),
                (qkv_s_hbm, qkv_s),
                (out_s_hbm, out_s),
                (qkv_t_hbm, qkv_t),
                (out_t_hbm, out_t),
            )
        )
    ]
    for load in loads:
        load.start()
    offsets = sorted(range(1, wide), key=lambda o: abs(o - wide // 2))
    barrier = pltpu.get_barrier_semaphore()
    for offset in offsets:
        pl.semaphore_signal(
            barrier, inc=1,
            device_id={"wide": lax.rem(me + offset, wide)}, device_id_type=MESH,
        )
    pl.semaphore_wait(barrier, wide - 1)

    def copy_one(frame, peer):
        return pltpu.make_async_remote_copy(
            src_ref=second.at[frame, peer],
            dst_ref=received.at[me * own + frame],
            send_sem=send_one.at[peer],
            recv_sem=recv_one.at[me],
            device_id={"wide": peer},
            device_id_type=MESH,
        )

    def whole_one(peer):
        return pltpu.make_async_remote_copy(
            src_ref=second.at[:, peer],
            dst_ref=received.at[pl.ds(peer * own, own)],
            send_sem=send_one.at[peer],
            recv_sem=recv_one.at[peer],
            device_id={"wide": peer},
            device_id_type=MESH,
        )

    def copy_two(pair, peer):
        return pltpu.make_async_remote_copy(
            src_ref=sending.at[pair, peer],
            dst_ref=returned.at[pair, me],
            send_sem=send_two.at[peer],
            recv_sem=recv_two.at[me],
            device_id={"wide": peer},
            device_id_type=MESH,
        )

    def whole_two(peer):
        return pltpu.make_async_remote_copy(
            src_ref=sending.at[:, peer],
            dst_ref=returned.at[:, peer],
            send_sem=send_two.at[peer],
            recv_sem=recv_two.at[peer],
            device_id={"wide": peer},
            device_id_type=MESH,
        )

    loads[0].wait()

    def norm_rows(floats):
        average = jnp.mean(floats, axis=-1, keepdims=True)
        centred = floats - average
        spread = jnp.mean(centred * centred, axis=-1, keepdims=True)
        return (centred * lax.rsqrt(spread + 1e-06)).astype(jnp.bfloat16)

    step_rows = 128

    def one_frame(frame, carry):
        def norm_first(i, c):
            rows = pl.ds(pl.multiple_of(i * step_rows, step_rows), step_rows)
            first[rows, :] = norm_rows(frames[frame, rows, :].astype(jnp.float32))
            return c

        lax.fori_loop(0, patches // step_rows, norm_first, 0, unroll=True)

        @pl.when(frame == 0)
        def _():
            loads[1].wait()

        def quad(c, carry):
            start = pl.multiple_of(c * 256, 256)
            tokens = first[...]
            queries = (dot32(tokens, qkv_s[:, pl.ds(start, 256)]) * scale).astype(jnp.bfloat16)
            key_part = dot32(
                tokens, qkv_s[:, pl.ds(pl.multiple_of(features + start, 256), 256)]
            ).astype(jnp.bfloat16)
            values = dot32(
                tokens, qkv_s[:, pl.ds(pl.multiple_of(2 * features + start, 256), 256)]
            ).astype(jnp.bfloat16)
            for half in range(2):
                cols = slice(128 * half, 128 * half + 128)
                mixed[:, pl.ds(pl.multiple_of(start + 128 * half, 128), 128)] = attend_pair(
                    queries[:, cols], key_part[:, cols], values[:, cols], None
                )
            return carry

        lax.fori_loop(0, features // 256, quad, 0, unroll=True)

        @pl.when(frame == 0)
        def _():
            loads[2].wait()

        def close(i, c):
            rows = pl.ds(pl.multiple_of(i * step_rows, step_rows), step_rows)
            update = dot32(mixed[rows, :], out_s[...])
            tokens = (frames[frame, rows, :].astype(jnp.float32) + update).astype(jnp.bfloat16)
            middle[frame, rows, :] = tokens
            normed = norm_rows(tokens.astype(jnp.float32))
            count = step_rows // per_group
            second[frame, pl.ds(i * count, count)] = normed.reshape(count, per_group, features)
            return c

        lax.fori_loop(0, patches // step_rows, close, 0, unroll=True)
        received[me * own + frame] = second[frame, me]
        for offset in offsets:
            copy_one(frame, lax.rem(me + offset, wide)).start()
        return carry

    lax.fori_loop(0, own, one_frame, 0)

    row = lax.broadcasted_iota(jnp.int32, (ROWS, ROWS), 0)
    col = lax.broadcasted_iota(jnp.int32, (ROWS, ROWS), 1)
    swap = jnp.where(
        (row // band == col % per_group) & (row % band == col // per_group), 1.0, 0.0
    ).astype(jnp.bfloat16)
    back = jnp.where(
        (col // band == row % per_group) & (col % band == row // per_group), 1.0, 0.0
    ).astype(jnp.bfloat16)
    few = 2
    span = few * band
    bias = jnp.where(
        (row[:, : few * bands * band] // band) % few == (col[:, : few * bands * band] // band) % few,
        0.0,
        -1e30,
    ).astype(jnp.float32)
    tall = bands * span

    def arrive(g, carry):
        for j in range(band // own):
            peer = g * (band // own) + j

            @pl.when(peer != me)
            def _():
                whole_one(peer).wait_recv()

        block = received[pl.ds(g * band, band)].reshape(ROWS, features)
        sorted_rows[g] = dot32(swap, block).astype(jnp.bfloat16)
        return carry

    lax.fori_loop(0, bands, arrive, 0)
    loads[3].wait()

    def pair_step(pair, carry):
        start = pl.multiple_of(pair * 128, 128)

        def project_band(g, c):
            tokens = sorted_rows[g]
            matrix = jnp.concatenate(
                [
                    qkv_t[:, pl.ds(pl.multiple_of(part * features + start, 128), 128)]
                    for part in range(3)
                ],
                axis=1,
            )
            out = dot32(tokens, matrix)
            heads_q[g] = (out[:, :128] * scale).astype(jnp.bfloat16)
            heads_k[g] = out[:, 128:256].astype(jnp.bfloat16)
            heads_v[g] = out[:, 256:].astype(jnp.bfloat16)
            return c

        lax.fori_loop(0, bands, project_band, 0, unroll=True)

        def batch(b, c):
            rows = pl.ds(pl.multiple_of(b * span, span), span)
            mix = attend_pair(
                heads_q[:, rows, :].reshape(tall, 128),
                heads_k[:, rows, :].reshape(tall, 128),
                heads_v[:, rows, :].reshape(tall, 128),
                bias,
            )
            temporal[:, rows, :] = mix.reshape(bands, span, 128)
            return c

        lax.fori_loop(0, per_group // few, batch, 0, unroll=True)
        peers = band // own

        def unsort(g, c):
            block = dot32(back, temporal[g]).astype(jnp.bfloat16)
            sending[pair, pl.ds(g * peers, peers)] = block.reshape(peers, own, per_group, 128)
            return c

        lax.fori_loop(0, bands, unsort, 0, unroll=True)
        returned[pair, me] = sending[pair, me]
        for offset in offsets:
            copy_two(pair, lax.rem(me + offset, wide)).start()
        return carry

    lax.fori_loop(0, pair_count, pair_step, 0)
    loads[4].wait()

    def settle(offset, carry):
        peer = lax.rem(me + offset, wide)
        whole_two(peer).wait_recv()
        return carry

    lax.fori_loop(1, wide, settle, 0)

    def finish(frame, carry):
        block = jnp.concatenate(
            [returned[pair, :, frame].reshape(patches, 128) for pair in range(pair_count)],
            axis=1,
        )
        change = dot32(block, out_t[...])
        result[frame] = (middle[frame].astype(jnp.float32) + change).astype(jnp.bfloat16)
        pltpu.make_async_copy(result.at[frame], result_hbm.at[frame], store_sem.at[frame]).start()
        return carry

    lax.fori_loop(0, own, finish, 0)

    def drain(offset, carry):
        peer = lax.rem(me + offset, wide)
        whole_one(peer).wait_send()
        whole_two(peer).wait_send()
        return carry

    lax.fori_loop(1, wide, drain, 0)

    def stored(frame, carry):
        pltpu.make_async_copy(result.at[frame], result_hbm.at[frame], store_sem.at[frame]).wait()
        return carry

    lax.fori_loop(0, own, stored, 0)


def fused(frames_in, qkv_spatial, out_spatial, qkv_temporal, out_temporal):
    own, patches, features = frames_in.shape
    wide = lax.axis_size("wide")
    per_group = patches // wide
    band = ROWS // per_group
    bands = own * wide // band
    pairs = features // 128
    bf16 = jnp.bfloat16
    vmem = pltpu.VMEM
    anywhere = pl.BlockSpec(memory_space=pl.ANY)
    return pl.pallas_call(
        functools.partial(kernel, wide),
        out_shape=jax.ShapeDtypeStruct(frames_in.shape, bf16),
        in_specs=[anywhere] * 5,
        out_specs=anywhere,
        scratch_shapes=[
            vmem(frames_in.shape, bf16),
            vmem(qkv_spatial.shape, bf16),
            vmem(out_spatial.shape, bf16),
            vmem(qkv_temporal.shape, bf16),
            vmem(out_temporal.shape, bf16),
            vmem((patches, features), bf16),
            vmem((patches, features), bf16),
            vmem((own, patches, features), bf16),
            vmem((own, wide, per_group, features), bf16),
            vmem((own * wide, per_group, features), bf16),
            vmem((bands, ROWS, features), bf16),
            vmem((bands, ROWS, 128), bf16),
            vmem((bands, ROWS, 128), bf16),
            vmem((bands, ROWS, 128), bf16),
            vmem((bands, ROWS, 128), bf16),
            vmem((pairs, wide, own, per_group, 128), bf16),
            vmem((pairs, wide, own, per_group, 128), bf16),
            vmem((own, patches, features), bf16),
            pltpu.SemaphoreType.DMA((5,)),
            pltpu.SemaphoreType.DMA((own,)),
            pltpu.SemaphoreType.DMA((wide,)),
            pltpu.SemaphoreType.DMA((wide,)),
            pltpu.SemaphoreType.DMA((wide,)),
            pltpu.SemaphoreType.DMA((wide,)),
        ],
        compiler_params=pltpu.CompilerParams(
            collective_id=0, has_side_effects=True, vmem_limit_bytes=60000 * 1024
        ),
    )(frames_in, qkv_spatial, out_spatial, qkv_temporal, out_temporal)


def fits(frames_in, wide):
    own, patches, features = frames_in.shape
    per_group = patches // wide
    if patches != ROWS or features % 256 or per_group % 16 or ROWS % per_group:
        return False
    band = ROWS // per_group
    return band % own == 0 and (own * wide) % band == 0 and per_group % (own * wide // band) == 0


def pick(frames_in, *matrices):
    if fits(frames_in, lax.axis_size("wide")):
        return fused(frames_in, *matrices)
    return shards(frames_in, *matrices)


def solution(mesh):
    return jax.shard_map(
        pick,
        mesh=mesh,
        in_specs=(P(("groups", "wide"), None, None), P(), P(), P(), P()),
        out_specs=P(("groups", "wide"), None, None),
        check_vma=False,
    )
```

```python
import functools

import jax
import jax.numpy as jnp
from jax import lax
from jax.experimental import pallas as pl
from jax.experimental.pallas import tpu as pltpu
from jax.sharding import PartitionSpec as P

HEADS = 12
HEAD_DIM = 64


def normalize(tensor):
    floats = tensor.astype(jnp.float32)
    average = jnp.mean(floats, axis=-1, keepdims=True)
    centred = floats - average
    spread = jnp.mean(centred * centred, axis=-1, keepdims=True)
    return (centred * lax.rsqrt(spread + 1e-06)).astype(jnp.bfloat16)


def project(flat_rows, matrix):
    return jnp.dot(flat_rows, matrix, preferred_element_type=jnp.float32)


def attend(projected, score_form, mix_form):
    leading = projected.shape[:-1]
    split = projected.reshape(leading + (3, HEADS, HEAD_DIM))
    queries = split[..., 0, :, :]
    key_part = split[..., 1, :, :]
    values = split[..., 2, :, :]
    scores = jnp.einsum(
        score_form, queries, key_part, preferred_element_type=jnp.float32
    ) * HEAD_DIM ** (-0.5)
    weights = jax.nn.softmax(scores, axis=-1).astype(jnp.bfloat16)
    mixed = jnp.einsum(mix_form, weights, values, preferred_element_type=jnp.float32)
    return mixed.reshape(leading + (HEADS * HEAD_DIM,)).astype(jnp.bfloat16)


def attend_time(received):
    frame_total, single, item_count, columns = received.shape
    sequences = received.reshape(frame_total, item_count, columns)
    result = attend(sequences, "qbhd,kbhd->bhqk", "bhqk,kbhd->qbhd")
    return result.reshape(frame_total, single, item_count, HEADS * HEAD_DIM)


def shards(frames_in, qkv_spatial, out_spatial, qkv_temporal, out_temporal):
    frame_count, patch_count, features = frames_in.shape
    wide_count = lax.axis_size("wide")
    per_group = patch_count // wide_count
    first = normalize(frames_in)
    proj_one = project(first.reshape(-1, features), qkv_spatial).astype(jnp.bfloat16)
    proj_one = proj_one.reshape(frame_count, patch_count, 3 * features)
    spatial = attend(proj_one, "bqhd,bkhd->bhqk", "bhqk,bkhd->bqhd")
    update = project(spatial.reshape(-1, features), out_spatial).reshape(
        frame_count, patch_count, features
    )
    middle = (frames_in.astype(jnp.float32) + update).astype(jnp.bfloat16)
    second = normalize(middle)
    grouped = second.reshape(frame_count, wide_count, per_group, features)
    received = lax.all_to_all(grouped, "wide", split_axis=1, concat_axis=0, tiled=True)
    frame_total, single, item_count, columns = received.shape
    local_proj = project(received.reshape(-1, columns), qkv_temporal).astype(jnp.bfloat16)
    local_proj = local_proj.reshape(frame_total, single, item_count, 3 * columns)
    temporal = attend_time(local_proj)
    returned = lax.all_to_all(temporal, "wide", split_axis=0, concat_axis=1, tiled=True)
    change = project(returned.reshape(-1, features), out_temporal).reshape(
        frame_count, patch_count, features
    )
    return (middle.astype(jnp.float32) + change).astype(jnp.bfloat16)

LOG2E = 1.4426950408889634
MESH = pl.DeviceIdType.MESH
ROWS = 256


def attend_pair(queries, key_part, values, bias):
    low = lax.broadcasted_iota(jnp.int32, queries.shape, 1) < HEAD_DIM
    zero = jnp.zeros_like(queries)
    stacked = jnp.concatenate(
        [jnp.where(low, queries, zero), jnp.where(low, zero, queries)], axis=0
    )
    scores = lax.dot_general(
        stacked, key_part, (((1,), (1,)), ((), ())), preferred_element_type=jnp.float32
    )
    if bias is not None:
        scores = scores + bias
    top = jnp.max(scores, axis=-1, keepdims=True)
    weights = jnp.exp2(scores - top).astype(jnp.bfloat16)
    both = dot32(weights, jnp.concatenate([values, jnp.ones_like(values)], axis=1))
    count = queries.shape[0]
    mixed = jnp.where(low, both[:count, :128], both[count:, :128])
    totals = jnp.where(low, both[:count, 128:], both[count:, 128:])
    return (mixed / totals).astype(jnp.bfloat16)


def dot32(a, b):
    return jnp.dot(a, b, preferred_element_type=jnp.float32)


def kernel(
    wide,
    frames_hbm, qkv_s_hbm, out_s_hbm, qkv_t_hbm, out_t_hbm,
    result_hbm,
    frames, qkv_s, out_s, qkv_t, out_t,
    first, mixed, middle, late, second, received, sorted_rows,
    heads_q, heads_k, heads_v, temporal, sending, returned, early, result,
    load_sem, store_sem, send_one, recv_one, send_two, recv_two,
):
    me = lax.axis_index("wide")
    own, patches, features = frames.shape
    group = patches // wide
    half = group // 2
    band = ROWS // group
    bands = own * wide // band
    peers = band // own
    height = half * band
    quads = features // 256
    scale = HEAD_DIM ** (-0.5) * LOG2E
    loads = [
        pltpu.make_async_copy(src, dst, load_sem.at[i])
        for i, (src, dst) in enumerate(
            (
                (frames_hbm, frames),
                (qkv_s_hbm, qkv_s),
                (out_s_hbm, out_s),
                (qkv_t_hbm, qkv_t),
                (out_t_hbm, out_t),
            )
        )
    ]
    loads[0].start()
    loads[1].start()
    offsets = range(1, wide)
    barrier = pltpu.get_barrier_semaphore()
    for offset in offsets:
        pl.semaphore_signal(
            barrier, inc=1,
            device_id={"wide": lax.rem(me + offset, wide)}, device_id_type=MESH,
        )
    pl.semaphore_wait(barrier, wide - 1)

    def copy_one(slot, peer, stage):
        return pltpu.make_async_remote_copy(
            src_ref=second.at[peer, slot],
            dst_ref=received.at[me, slot],
            send_sem=send_one.at[stage, peer],
            recv_sem=recv_one.at[stage, me],
            device_id={"wide": peer},
            device_id_type=MESH,
        )

    def whole_one(peer, stage):
        slots = pl.ds(0, own - 1) if stage == 0 else pl.ds(own - 1, 1)
        return pltpu.make_async_remote_copy(
            src_ref=second.at[peer, slots],
            dst_ref=received.at[peer, slots],
            send_sem=send_one.at[stage, peer],
            recv_sem=recv_one.at[stage, peer],
            device_id={"wide": peer},
            device_id_type=MESH,
        )

    def copy_two(stage, quad, peer):
        return pltpu.make_async_remote_copy(
            src_ref=sending.at[stage, peer, quad],
            dst_ref=returned.at[stage, me, quad],
            send_sem=send_two.at[stage, peer],
            recv_sem=recv_two.at[stage, me],
            device_id={"wide": peer},
            device_id_type=MESH,
        )

    def whole_two(stage, peer):
        return pltpu.make_async_remote_copy(
            src_ref=sending.at[stage, peer],
            dst_ref=returned.at[stage, peer],
            send_sem=send_two.at[stage, peer],
            recv_sem=recv_two.at[stage, peer],
            device_id={"wide": peer},
            device_id_type=MESH,
        )

    loads[0].wait()

    def norm_rows(floats):
        average = jnp.mean(floats, axis=-1, keepdims=True)
        centred = floats - average
        spread = jnp.mean(centred * centred, axis=-1, keepdims=True)
        return centred * lax.rsqrt(spread + 1e-06)

    step_rows = 128

    def spatial_frame(frame, keep):
        def norm_first(i, c):
            rows = pl.ds(pl.multiple_of(i * step_rows, step_rows), step_rows)
            first[rows, :] = norm_rows(frames[frame, rows, :].astype(jnp.float32)).astype(jnp.bfloat16)
            return c

        lax.fori_loop(0, patches // step_rows, norm_first, 0, unroll=True)

        @pl.when(frame == 0)
        def _():
            loads[1].wait()
            for load in loads[2:]:
                load.start()

        def quad_step(c, carry):
            start = pl.multiple_of(c * 256, 256)
            tokens = first[...]
            queries = (dot32(tokens, qkv_s[:, pl.ds(start, 256)]) * scale).astype(jnp.bfloat16)
            key_part = dot32(
                tokens, qkv_s[:, pl.ds(pl.multiple_of(features + start, 256), 256)]
            ).astype(jnp.bfloat16)
            values = dot32(
                tokens, qkv_s[:, pl.ds(pl.multiple_of(2 * features + start, 256), 256)]
            ).astype(jnp.bfloat16)
            for part in range(2):
                cols = slice(128 * part, 128 * part + 128)
                mixed[:, pl.ds(pl.multiple_of(start + 128 * part, 128), 128)] = attend_pair(
                    queries[:, cols], key_part[:, cols], values[:, cols], None
                )
            return carry

        lax.fori_loop(0, quads, quad_step, 0, unroll=True)

        @pl.when(frame == 0)
        def _():
            loads[2].wait()

        def close(i, c):
            rows = pl.ds(pl.multiple_of(i * step_rows, step_rows), step_rows)
            update = dot32(mixed[rows, :], out_s[...])
            tokens = (frames[frame, rows, :].astype(jnp.float32) + update).astype(jnp.bfloat16)
            middle[frame, rows, :] = tokens
            keep(i, rows, norm_rows(tokens.astype(jnp.float32)))
            return c

        lax.fori_loop(0, patches // step_rows, close, 0, unroll=True)

    def send_slot(slot, stage):
        received[me, slot] = second[me, slot]
        for offset in offsets:
            copy_one(slot, lax.rem(me + offset, wide), stage).start()

    def whole_frame(frame, carry):
        def keep(i, rows, normed):
            count = step_rows // group
            second[pl.ds(i * count, count), frame] = normed.astype(jnp.bfloat16).reshape(
                count, group, features
            )

        spatial_frame(frame, keep)
        send_slot(frame, 0)
        return carry

    lax.fori_loop(0, own - 2, whole_frame, 0)

    def late_frame(place, carry):
        def keep(i, rows, normed):
            late[place, rows, :] = normed

        spatial_frame(own - 2 + place, keep)
        return carry

    lax.fori_loop(0, 2, late_frame, 0)

    for stage in range(2):
        parts = [
            late[place].reshape(wide, 2, half, features)[:, stage : stage + 1] for place in range(2)
        ]
        unit = jnp.concatenate(parts, axis=1).reshape(wide, group, features)
        second[:, own - 2 + stage] = unit.astype(jnp.bfloat16)
        send_slot(own - 2 + stage, stage)

    depth = peers * (own - 1) * group

    def sorter(stage):
        row = lax.broadcasted_iota(jnp.int32, (height, depth), 0)
        col = lax.broadcasted_iota(jnp.int32, (height, depth), 1)
        patch, frame = row // band, row % band
        local = frame % own
        inside = jnp.where(
            local < own - 2,
            local * group + stage * half + patch,
            (own - 2) * group + (local - (own - 2)) * half + patch,
        )
        target = (frame // own) * ((own - 1) * group) + inside
        return jnp.where(col == target, 1.0, 0.0).astype(jnp.bfloat16)

    row = lax.broadcasted_iota(jnp.int32, (height, height), 0)
    col = lax.broadcasted_iota(jnp.int32, (height, height), 1)
    back = jnp.where(col == (row % half) * band + row // half, 1.0, 0.0).astype(jnp.bfloat16)
    few = 2
    span = few * band
    tall = bands * span
    tall_row = lax.broadcasted_iota(jnp.int32, (2 * tall, tall), 0)
    tall_col = lax.broadcasted_iota(jnp.int32, (2 * tall, tall), 1)
    bias = jnp.where(
        (tall_row // band) % few == (tall_col // band) % few, 0.0, -1e30
    ).astype(jnp.float32)

    for stage in range(2):
        swap = sorter(stage)

        def arrive(g, carry):
            for j in range(peers):
                peer = g * peers + j

                @pl.when(peer != me)
                def _():
                    whole_one(peer, stage).wait_recv()

            if stage == 0:
                block = received[pl.ds(g * peers, peers), : own - 1]
            else:
                block = jnp.concatenate(
                    [
                        received[pl.ds(g * peers, peers), : own - 2],
                        received[pl.ds(g * peers, peers), own - 1 :],
                    ],
                    axis=1,
                )
            sorted_rows[g] = dot32(swap, block.reshape(depth, features)).astype(jnp.bfloat16)
            return carry

        lax.fori_loop(0, bands, arrive, 0)
        if stage == 0:
            loads[3].wait()

        def quad_time(quad, carry):
            start = pl.multiple_of(quad * 256, 256)
            for g in range(0, bands, 2):
                tokens = sorted_rows[g : g + 2].reshape(2 * height, features)
                for part, target in enumerate((heads_q, heads_k, heads_v)):
                    out = dot32(
                        tokens, qkv_t[:, pl.ds(pl.multiple_of(part * features + start, 256), 256)]
                    )
                    if part == 0:
                        out = out * scale
                    target[g : g + 2] = out.astype(jnp.bfloat16).reshape(2, height, 256)
            for b in range(half // few):
                rows = slice(b * span, b * span + span)
                for part in range(2):
                    cols = slice(128 * part, 128 * part + 128)
                    mix = attend_pair(
                        heads_q[:, rows, cols].reshape(tall, 128),
                        heads_k[:, rows, cols].reshape(tall, 128),
                        heads_v[:, rows, cols].reshape(tall, 128),
                        bias,
                    )
                    temporal[:, rows, cols] = mix.reshape(bands, span, 128)
            for g in range(bands):
                block = dot32(back, temporal[g]).astype(jnp.bfloat16)
                sending[stage, g * peers : (g + 1) * peers, quad] = block.reshape(
                    peers, own // 2, group, 256
                )
            returned[stage, me, quad] = sending[stage, me, quad]
            for offset in offsets:
                copy_two(stage, quad, lax.rem(me + offset, wide)).start()
            return carry

        lax.fori_loop(0, quads, quad_time, 0)

    loads[4].wait()
    for stage in range(2):

        def settle(offset, carry):
            whole_two(stage, lax.rem(me + offset, wide)).wait_recv()
            return carry

        lax.fori_loop(1, wide, settle, 0)
        for tile in range(own // 2):
            block = jnp.concatenate(
                [returned[stage, :, quad, tile].reshape(patches, 256) for quad in range(quads)],
                axis=1,
            )
            change = dot32(block, out_t[...])
            if stage == 0:
                early[tile] = change
                continue
            whole = [part.reshape(wide, 2, half, features) for part in (early[tile], change)]
            for place in range(2):
                frame = 2 * tile + place
                update = jnp.concatenate(
                    [part[:, place : place + 1] for part in whole], axis=1
                ).reshape(patches, features)
                result[frame] = (middle[frame].astype(jnp.float32) + update).astype(jnp.bfloat16)
                pltpu.make_async_copy(
                    result.at[frame], result_hbm.at[frame], store_sem.at[frame]
                ).start()

    def drain(offset, carry):
        peer = lax.rem(me + offset, wide)
        for stage in range(2):
            whole_one(peer, stage).wait_send()
            whole_two(stage, peer).wait_send()
        return carry

    lax.fori_loop(1, wide, drain, 0)

    def stored(frame, carry):
        pltpu.make_async_copy(result.at[frame], result_hbm.at[frame], store_sem.at[frame]).wait()
        return carry

    lax.fori_loop(0, own, stored, 0)


def fused(frames_in, qkv_spatial, out_spatial, qkv_temporal, out_temporal):
    own, patches, features = frames_in.shape
    wide = lax.axis_size("wide")
    group = patches // wide
    band = ROWS // group
    bands = own * wide // band
    height = (group // 2) * band
    quads = features // 256
    bf16 = jnp.bfloat16
    vmem = pltpu.VMEM
    anywhere = pl.BlockSpec(memory_space=pl.ANY)
    return pl.pallas_call(
        functools.partial(kernel, wide),
        out_shape=jax.ShapeDtypeStruct(frames_in.shape, bf16),
        in_specs=[anywhere] * 5,
        out_specs=anywhere,
        scratch_shapes=[
            vmem(frames_in.shape, bf16),
            vmem(qkv_spatial.shape, bf16),
            vmem(out_spatial.shape, bf16),
            vmem(qkv_temporal.shape, bf16),
            vmem(out_temporal.shape, bf16),
            vmem((patches, features), bf16),
            vmem((patches, features), bf16),
            vmem((own, patches, features), bf16),
            vmem((2, patches, features), jnp.float32),
            vmem((wide, own, group, features), bf16),
            vmem((wide, own, group, features), bf16),
            vmem((bands, height, features), bf16),
            vmem((bands, height, 256), bf16),
            vmem((bands, height, 256), bf16),
            vmem((bands, height, 256), bf16),
            vmem((bands, height, 256), bf16),
            vmem((2, wide, quads, own // 2, group, 256), bf16),
            vmem((2, wide, quads, own // 2, group, 256), bf16),
            vmem((own // 2, patches, features), jnp.float32),
            vmem((own, patches, features), bf16),
            pltpu.SemaphoreType.DMA((5,)),
            pltpu.SemaphoreType.DMA((own,)),
            pltpu.SemaphoreType.DMA((2, wide)),
            pltpu.SemaphoreType.DMA((2, wide)),
            pltpu.SemaphoreType.DMA((2, wide)),
            pltpu.SemaphoreType.DMA((2, wide)),
        ],
        compiler_params=pltpu.CompilerParams(
            collective_id=0, has_side_effects=True, vmem_limit_bytes=60000 * 1024
        ),
    )(frames_in, qkv_spatial, out_spatial, qkv_temporal, out_temporal)


def fits(frames_in, wide):
    own, patches, features = frames_in.shape
    if patches != ROWS or features % 256 or patches % wide or patches // wide != 16:
        return False
    band = ROWS // 16
    return own == 4 and (own * wide) % (2 * band) == 0


def pick(frames_in, *matrices):
    if fits(frames_in, lax.axis_size("wide")):
        return fused(frames_in, *matrices)
    return shards(frames_in, *matrices)


def solution(mesh):
    return jax.shard_map(
        pick,
        mesh=mesh,
        in_specs=(P(("groups", "wide"), None, None), P(), P(), P(), P()),
        out_specs=P(("groups", "wide"), None, None),
        check_vma=False,
    )
```
